32 devices in a mesh: dp: 4 (over y, x), seq: 2 (over core), tensor: 4 (over z).
Axes of the slice: x: 2, y: 2, z: 4, core: 2. Of those that a mesh axis runs over, the one named last changes fastest.
Arguments:
- block_input: float32 [4, 16, 256, 1024], P('dp', 'seq', 'tensor'), may hold values from -6 to 6
- w_qkv: bfloat16 [1024, 3, 1024], P(None, None, 'tensor'), may hold values from -0.1875 to 0.1875
- qv_bias: bfloat16 [2, 1024], P(None, 'tensor'), may hold values from -3 to 3
- w_out: bfloat16 [1024, 1024], P('tensor'), may hold values from -3 to 3
- b_out: bfloat16 [1024], replicated, may hold values from -3 to 3
- w_up: bfloat16 [1024, 4096], P(None, 'tensor'), may hold values from -0.1875 to 0.1875
- b_up: bfloat16 [4096], P('tensor'), may hold values from -3 to 3
- w_down: bfloat16 [4096, 1024], P('tensor'), may hold values from -0.09375 to 0.09375
- b_down: bfloat16 [1024], replicated, may hold values from -3 to 3
- w_mod: bfloat16 [1024, 6144], replicated, may hold values from -0.375 to 0.375
- b_mod: bfloat16 [6144], replicated, may hold values from -3 to 3
- context_frames: int32 [4], P('dp'), may hold values from 1 to 15
- noise_levels: int32 [4, 16], P('dp', 'seq'), may hold values from 0 to 999
- cotangent: float32 [4, 16, 256, 1024], P('dp', 'seq', 'tensor'), may hold values from -6 to 6
Outputs:
- output: float32 [4, 16, 256, 1024], P('dp', 'seq', 'tensor')
- grad_input: float32 [4, 16, 256, 1024], P('dp', 'seq', 'tensor')
- grad_w_qkv: float32 [1024, 3, 1024], P(None, None, 'tensor')
- grad_qv_bias: float32 [2, 1024], P(None, 'tensor')
- grad_w_out: float32 [1024, 1024], P('tensor')
- grad_b_out: float32 [1024], P('tensor')
- grad_w_up: float32 [1024, 4096], P(None, 'tensor')
- grad_b_up: float32 [4096], P('tensor')
- grad_w_down: float32 [4096, 1024], P('tensor')
- grad_b_down: float32 [1024], P('tensor')
- grad_w_mod: float32 [1024, 6144], P(None, 'tensor')
- grad_b_mod: float32 [6144], P('tensor')
The draws below stay inside these ranges and needn't reach their ends.
Inputs may be any that keep to these rules, and one draw needn't show every extreme that they name: `noise_levels`: noise level index of each frame.
All inputs are finite; a program needn't handle non-finite values.
Results may differ from the reference program's by a relative error of at most 0.02.
Values may be sent and summed in bfloat16 or wider, within the bound.
No kernel may reach another device: no remote copies, remote signals or barrier semaphores. Data moves between devices by JAX's collectives and lax.ppermute only.
A program may use at most 256 MiB of HBM per device.

```python
import math
import jax
import jax.numpy as jnp
from jax import lax

D = 1024
HEADS = 16
HD = 64
FF = 4096
FRAMES = 16
PATCHES = 256
LEVELS = 1000
CLIPS = 4
N_TENSOR = 4


def place_ends(array, rng, low, top_value):
    longest = array.shape.index(max(array.shape))
    spots = []
    for shift in (0, 1):
        where = [jax.random.randint(jax.random.fold_in(rng, axis), (), 0, length) for axis, length in enumerate(array.shape)]
        where[longest] = (where[longest] + shift) % array.shape[longest]
        spots.append(tuple(where))
    return array.at[spots[0]].set(low).at[spots[1]].set(top_value)


def steps_of(key, shape, cuts, low, high):
    def one(position, parts):
        steps = jax.random.uniform(jax.random.fold_in(jax.random.fold_in(key, 6), position), (parts,), jnp.float32, low / len(cuts), high / len(cuts))
        return jnp.repeat(jnp.exp(steps), shape[position] // parts).reshape((-1,) + (1,) * (len(shape) - position - 1))

    level = one(*cuts[0])
    for cut in cuts[1:]:
        level = level * one(*cut)
    return level


def centred(stream_key, shape, scale, most, cuts=(), kind=jnp.bfloat16):
    loudness = steps_of(stream_key, shape, cuts, -0.22, 0.18) if cuts else 1.0
    drawn = jax.random.normal(stream_key, shape, jnp.float32) * scale * loudness
    return jnp.minimum(jnp.maximum(drawn, -most), most).astype(kind)


def setup_inputs(seed: int = 0) -> dict:
    arg_keys = jax.random.split(jax.random.key(seed), 15)
    return {
        "block_input": centred(arg_keys[0], (CLIPS, FRAMES, PATCHES, D), 1.0, 6.0, ((0, 4), (1, 2), (2, 4)), jnp.float32),
        "w_qkv": centred(arg_keys[1], (D, 3, D), D ** -0.5, 0.1875, ((2, 4),)),
        "qv_bias": centred(arg_keys[2], (2, D), 0.5, 3.0, ((1, 4),)),
        "w_out": centred(arg_keys[3], (D, D), (max(D // 256, 4)) ** -0.5, 3.0, ((0, 4),)),
        "b_out": centred(arg_keys[4], (D,), 0.5, 3.0),
        "w_up": centred(arg_keys[5], (D, FF), D ** -0.5, 0.1875, ((1, 4),)),
        "b_up": centred(arg_keys[6], (FF,), 0.5, 3.0, ((0, 4),)),
        "w_down": centred(arg_keys[7], (FF, D), FF ** -0.5, 0.09375, ((0, 4),)),
        "b_down": centred(arg_keys[8], (D,), 0.5, 3.0),
        "w_mod": centred(arg_keys[9], (D, 6 * D), (D // 4) ** -0.5, 0.375),
        "b_mod": centred(arg_keys[10], (6 * D,), 0.5, 3.0),
        "context_frames": place_ends(jax.random.randint(arg_keys[11], (CLIPS,), 1, FRAMES), jax.random.fold_in(arg_keys[11], 1), 1, FRAMES - 1).astype(jnp.int32),
        "noise_levels": place_ends(jax.random.randint(arg_keys[12], (CLIPS, FRAMES), 0, LEVELS), jax.random.fold_in(arg_keys[12], 1), 0, LEVELS - 1).astype(jnp.int32),
        "cotangent": centred(arg_keys[13], (CLIPS, FRAMES, PATCHES, D), 1.0, 6.0, ((0, 4), (1, 2), (2, 4)), jnp.float32),
    }


@jax.custom_vjp
def low(v):
    return lax.optimization_barrier(v.astype(jnp.bfloat16)).astype(jnp.float32)

@jax.custom_vjp
def low_back(v):
    return v

def low_keep(v):
    return (low(v), None)

def low_pass(kept, grad):
    return (grad,)

def back_keep(v):
    return (v, None)

def back_low(kept, grad):
    return (low(grad),)
low.defvjp(low_keep, low_pass)
low_back.defvjp(back_keep, back_low)

def level_features(levels, context, frame_ids, breadth):
    level_used = jnp.where(frame_ids[None, :] < context[:, None], 0, levels).astype(jnp.float32)
    halfway = breadth // 2
    frequency = jnp.exp(-math.log(10000.0) * jnp.arange(halfway, dtype=jnp.float32) / halfway)
    angles = level_used[..., None] * frequency
    return jax.nn.silu(jnp.concatenate([jnp.cos(angles), jnp.sin(angles)], axis=-1))

def normalize(stream):
    centre = stream - lax.optimization_barrier(jnp.mean(stream, axis=-1, keepdims=True))
    inverse = lax.rsqrt(lax.optimization_barrier(jnp.mean(centre * centre, axis=-1, keepdims=True)) + 1e-06)
    return centre * inverse

def row_groups(left, weight):
    width = left.shape[-1] // N_TENSOR
    total = None
    for group in range(N_TENSOR):
        part = jnp.einsum('cfpe,ed->cfpd', left[..., group * width:(group + 1) * width], weight[group * width:(group + 1) * width], precision=lax.Precision.HIGHEST)
        part = low(part)
        total = part if total is None else total + part
    return total

def column_groups(left, weight, form):
    width = weight.shape[-1] // N_TENSOR
    pieces = []
    for group in range(N_TENSOR):
        pieces.append(jnp.einsum(form, low_back(left), weight[..., group * width:(group + 1) * width], precision=lax.Precision.HIGHEST))
    return jnp.concatenate(pieces, axis=-1)

def attend_clip(members):
    queries, keys, values, context = members
    length = FRAMES * PATCHES
    query_heads = queries.reshape(length, HEADS, HD).transpose(1, 0, 2)
    key_heads = keys.reshape(length, HEADS, HD).transpose(1, 0, 2)
    value_heads = values.reshape(length, HEADS, HD).transpose(1, 0, 2)
    frame_of = jnp.arange(length, dtype=jnp.int32) // PATCHES
    allowed = (frame_of[None, :] <= frame_of[:, None]) | (frame_of[None, :] < context)

    def one_head(slices):
        query_one, key_one, value_one = slices
        scores = low_back(jnp.dot(query_one, key_one.T, precision=lax.Precision.HIGHEST) * HD ** (-0.5))
        scores = jnp.where(allowed, scores, -1e+30)
        probability = jax.nn.softmax(scores, axis=-1)
        return jnp.dot(low(probability), value_one, precision=lax.Precision.HIGHEST)
    result = lax.map(jax.checkpoint(one_head), (query_heads, key_heads, value_heads))
    return result.transpose(1, 0, 2).reshape(FRAMES, PATCHES, D)

def reference(block_input, w_qkv, qv_bias, w_out, b_out, w_up, b_up, w_down, b_down, w_mod, b_mod, context_frames, noise_levels, cotangent):
    frame_ids = jnp.arange(FRAMES, dtype=jnp.int32)
    condition = low(level_features(noise_levels, context_frames, frame_ids, D))
    exact = lax.Precision.HIGHEST

    def forward(stream, weight_qkv, bias_qv, weight_out, bias_out, weight_up, bias_up, weight_down, bias_down, weight_mod, bias_mod):
        modulation = jnp.einsum('cfd,de->cfe', condition, weight_mod, precision=exact) + bias_mod
        shift_one, scale_one, gate_one, shift_two, scale_two, gate_two = jnp.split(modulation[:, :, None, :], 6, axis=-1)
        attn_in = low(normalize(stream) * (1.0 + scale_one) + shift_one)
        projected = column_groups(attn_in, weight_qkv, 'cfpd,dke->cfpke')
        queries = low_back(low(projected[..., 0, :] + bias_qv[0]))
        keys = low_back(low(projected[..., 1, :]))
        values = low_back(low(projected[..., 2, :] + bias_qv[1]))
        attended = low_back(low(lax.map(jax.checkpoint(attend_clip), (queries, keys, values, context_frames))))
        branch = low_back(row_groups(attended, weight_out)) + bias_out
        hidden_one = stream + gate_one * branch
        mlp_in = low(normalize(hidden_one) * (1.0 + scale_two) + shift_two)
        pre_act = low_back(column_groups(mlp_in, weight_up, 'cfpd,de->cfpe') + bias_up)
        activated = low(jax.nn.gelu(pre_act, approximate=True))
        mlp_out = low_back(row_groups(activated, weight_down)) + bias_down
        return hidden_one + gate_two * mlp_out
    output, pullback = jax.vjp(forward, block_input, w_qkv.astype(jnp.float32), qv_bias.astype(jnp.float32), w_out.astype(jnp.float32), b_out.astype(jnp.float32), w_up.astype(jnp.float32), b_up.astype(jnp.float32), w_down.astype(jnp.float32), b_down.astype(jnp.float32), w_mod.astype(jnp.float32), b_mod.astype(jnp.float32))
    grad_input, grad_w_qkv, grad_qv_bias, grad_w_out, grad_b_out, grad_w_up, grad_b_up, grad_w_down, grad_b_down, grad_w_mod, grad_b_mod = pullback(cotangent)
    return (output, grad_input, grad_w_qkv, grad_qv_bias, grad_w_out, grad_b_out, grad_w_up, grad_b_up, grad_w_down, grad_b_down, grad_w_mod, grad_b_mod)
```

```python
import functools
import math

import jax
import jax.numpy as jnp
from jax import lax
from jax.experimental import pallas as pl
from jax.experimental.pallas import tpu as pltpu
from jax.sharding import PartitionSpec as P

HD = 64
F32 = jnp.float32
BF = jnp.bfloat16
NT=(((1,),(1,)),((),()))
def split_heads(block, out_ref, rows, heads):
    lane=lax.broadcasted_iota(jnp.int32, block.shape, 1)//HD
    for h in range(heads):
        out_ref[h*rows:(h+1)*rows,:]=jnp.where(lane==h, block, jnp.zeros_like(block))
def fwd_kernel(rows, heads, frames, nvis_ref, q_ref, k_ref, v_ref, o_ref, p_ref, linv_ref, vt_ref, s_ref, b_ref, acc_ref):
    c=pl.program_id(0); i=pl.program_id(1)
    total=k_ref.shape[1]
    cols=q_ref.shape[2]
    @pl.when(i==0)
    def _():
        @pl.loop(0,total//rows)
        def _(j):
            at=pl.ds(pl.multiple_of(j*rows,rows),rows)
            vt_ref[:,at]=v_ref[0,at,:].T
    n=nvis_ref[c*frames+i]
    split_heads(q_ref[0]*jnp.asarray(HD**-0.5,BF), b_ref, rows, heads)
    wide=heads*rows
    def scan_scores(j, top):
        at=pl.ds(pl.multiple_of(j*rows,rows),rows)
        s=lax.dot_general(k_ref[0,at,:], b_ref[...], NT, preferred_element_type=F32)
        s_ref[at,:]=s
        return jnp.maximum(top, jnp.max(s.reshape(rows//8,8,wide),axis=0))
    top=lax.fori_loop(0,n,scan_scores,jnp.full((8,wide),-jnp.inf,F32))
    top=jnp.max(top,axis=0,keepdims=True)
    acc_ref[...]=jnp.zeros_like(acc_ref)
    def gather_values(j, mass):
        at=pl.ds(pl.multiple_of(j*rows,rows),rows)
        p=jnp.exp(s_ref[at,:]-top)
        low=p.astype(BF)
        p_ref[0,0,at,:]=low
        for h in range(heads):
            acc_ref[h*HD:(h+1)*HD,:]+=jnp.dot(vt_ref[h*HD:(h+1)*HD,at], low[:,h*rows:(h+1)*rows], preferred_element_type=F32)
        return mass+jnp.sum(p.reshape(rows//8,8,wide),axis=0)
    mass=lax.fori_loop(0,n,gather_values,jnp.zeros((8,wide),F32))
    inv=1.0/jnp.sum(mass,axis=0,keepdims=True)
    full=jnp.concatenate([jnp.broadcast_to(inv[:,h*rows:(h+1)*rows],(HD,rows)) for h in range(heads)],axis=0)
    o_ref[0]=(acc_ref[...]*full).T.astype(BF)
    linv_ref[0]=full.T
def attn_fwd(nvis,q,k,v,rows):
    C,Q,cols=q.shape; heads=cols//HD; frames=Q//rows; K=k.shape[1]
    wide=heads*rows
    qspec=pl.BlockSpec((1,rows,cols),lambda c,i,n:(c,i,0))
    kspec=pl.BlockSpec((1,K,cols),lambda c,i,n:(c,0,0))
    return pl.pallas_call(functools.partial(fwd_kernel,rows,heads,frames),
      grid_spec=pltpu.PrefetchScalarGridSpec(num_scalar_prefetch=1,grid=(C,frames),
        in_specs=[qspec,kspec,kspec],
        out_specs=[qspec,pl.BlockSpec((1,1,K,wide),lambda c,i,n:(c,i,0,0)),qspec],
        scratch_shapes=[pltpu.VMEM((cols,K),BF),pltpu.VMEM((K,wide),F32),pltpu.VMEM((wide,cols),BF),pltpu.VMEM((cols,rows),F32)]),
      out_shape=[jax.ShapeDtypeStruct(q.shape,BF),jax.ShapeDtypeStruct((C,frames,K,wide),BF),jax.ShapeDtypeStruct(q.shape,F32)],
      compiler_params=pltpu.CompilerParams(vmem_limit_bytes=60<<20),
      name="attend_forward")(nvis,q,k,v)
def bwd_kernel(rows, heads, frames, nvis_ref, q_ref, k_ref, v_ref, o_ref, do_ref, linv_ref, p_ref, dq_ref, dk_ref, dv_ref, kt_ref, bq_ref, bd_ref, dka_ref, dva_ref, dqt_ref):
    c=pl.program_id(0); i=pl.program_id(1)
    total=k_ref.shape[1]
    @pl.when(i==0)
    def _():
        @pl.loop(0,total//rows)
        def _(j):
            at=pl.ds(pl.multiple_of(j*rows,rows),rows)
            kt_ref[:,at]=k_ref[0,at,:].T
            dka_ref[at,:]=jnp.zeros((rows,dka_ref.shape[1]),F32)
            dva_ref[at,:]=jnp.zeros((rows,dka_ref.shape[1]),F32)
    n=nvis_ref[c*frames+i]
    split_heads(q_ref[0]*jnp.asarray(HD**-0.5,BF), bq_ref, rows, heads)
    scaled=do_ref[0].astype(F32)*linv_ref[0]
    split_heads(scaled.astype(BF), bd_ref, rows, heads)
    prod=(scaled*o_ref[0].astype(F32)).T
    delta=jnp.concatenate([jnp.sum(prod[h*HD:(h+1)*HD],axis=0,keepdims=True) for h in range(heads)],axis=1)
    dqt_ref[...]=jnp.zeros_like(dqt_ref)
    @pl.loop(0,n)
    def _(j):
        at=pl.ds(pl.multiple_of(j*rows,rows),rows)
        dp=lax.dot_general(v_ref[0,at,:], bd_ref[...], NT, preferred_element_type=F32)
        low=p_ref[0,0,at,:]
        ds=(low.astype(F32)*(dp-delta)).astype(BF)
        dva_ref[at,:]+=jnp.dot(low,bd_ref[...],preferred_element_type=F32)
        dka_ref[at,:]+=jnp.dot(ds,bq_ref[...],preferred_element_type=F32)
        for h in range(heads):
            dqt_ref[h*HD:(h+1)*HD,:]+=jnp.dot(kt_ref[h*HD:(h+1)*HD,at], ds[:,h*rows:(h+1)*rows], preferred_element_type=F32)
    dq_ref[0]=(dqt_ref[...].T*HD**-0.5).astype(BF)
    @pl.when(i==frames-1)
    def _():
        @pl.loop(0,total//rows)
        def _(j):
            at=pl.ds(pl.multiple_of(j*rows,rows),rows)
            dk_ref[0,at,:]=dka_ref[at,:].astype(BF)
            dv_ref[0,at,:]=dva_ref[at,:].astype(BF)
def attn_bwd(nvis,q,k,v,o,do,linv,p,rows):
    C,Q,cols=q.shape; heads=cols//HD; frames=Q//rows; K=k.shape[1]
    wide=heads*rows
    qspec=pl.BlockSpec((1,rows,cols),lambda c,i,n:(c,i,0))
    kspec=pl.BlockSpec((1,K,cols),lambda c,i,n:(c,0,0))
    return pl.pallas_call(functools.partial(bwd_kernel,rows,heads,frames),
      grid_spec=pltpu.PrefetchScalarGridSpec(num_scalar_prefetch=1,grid=(C,frames),
        in_specs=[qspec,kspec,kspec,qspec,qspec,qspec,pl.BlockSpec((1,1,K,wide),lambda c,i,n:(c,i,0,0))],
        out_specs=[qspec,kspec,kspec],
        scratch_shapes=[pltpu.VMEM((cols,K),BF),pltpu.VMEM((wide,cols),BF),pltpu.VMEM((wide,cols),BF),pltpu.VMEM((K,cols),F32),pltpu.VMEM((K,cols),F32),pltpu.VMEM((cols,rows),F32)]),
      out_shape=[jax.ShapeDtypeStruct(q.shape,BF),jax.ShapeDtypeStruct(k.shape,BF),jax.ShapeDtypeStruct(k.shape,BF)],
      compiler_params=pltpu.CompilerParams(vmem_limit_bytes=60<<20),
      name="attend_backward")(nvis,q,k,v,o,do,linv,p)


def level_features(levels, context, frame_ids, breadth):
    level_used = jnp.where(frame_ids[None, :] < context[:, None], 0, levels).astype(jnp.float32)
    halfway = breadth // 2
    frequency = jnp.exp(-math.log(10000.0) * jnp.arange(halfway, dtype=jnp.float32) / halfway)
    angles = level_used[..., None] * frequency
    return jax.nn.silu(jnp.concatenate([jnp.cos(angles), jnp.sin(angles)], axis=-1))


def normalize(stream):
    centre = stream - jnp.mean(stream, axis=-1, keepdims=True)
    inverse = lax.rsqrt(jnp.mean(centre * centre, axis=-1, keepdims=True) + 1e-06)
    return (centre * inverse, inverse)


def norm_back(grad_normed, normed, inverse):
    first_mean = jnp.mean(grad_normed, axis=-1, keepdims=True)
    second_mean = jnp.mean(grad_normed * normed, axis=-1, keepdims=True)
    return inverse * (grad_normed - first_mean - normed * second_mean)


def gelu_back(pre_act, grad_act):
    _, pullback = jax.vjp(lambda argument: jax.nn.gelu(argument, approximate=True), pre_act)
    return pullback(grad_act)[0]


def body(
    block_input,
    w_qkv,
    qv_bias,
    w_out,
    b_out,
    w_up,
    b_up,
    w_down,
    b_down,
    w_mod,
    b_mod,
    context_frames,
    noise_levels,
    cotangent,
):
    clip_count, half_frames, patch_local, breadth = block_input.shape
    patches_all = patch_local * lax.axis_size("tensor")
    head_cols = w_qkv.shape[2]
    frame_first = lax.axis_index("seq") * half_frames
    frame_ids = frame_first + jnp.arange(half_frames, dtype=jnp.int32)
    condition = level_features(noise_levels, context_frames, frame_ids, breadth).astype(
        jnp.bfloat16
    )
    modulation = jnp.einsum(
        "cfd,de->cfe", condition, w_mod, preferred_element_type=jnp.float32
    ) + b_mod.astype(jnp.float32)
    shift_one, scale_one, gate_one, shift_two, scale_two, gate_two = jnp.split(
        modulation[:, :, None, :], 6, axis=-1
    )
    normed_one, inverse_one = normalize(block_input)
    attn_in = (normed_one * (1.0 + scale_one) + shift_one).astype(jnp.bfloat16)
    attn_all = lax.all_gather(attn_in, "tensor", axis=2, tiled=True)
    projected = jnp.einsum("cfpd,dke->cfpke", attn_all, w_qkv, preferred_element_type=jnp.float32)
    bias_float = qv_bias.astype(jnp.float32)
    queries = (projected[..., 0, :] + bias_float[0]).astype(jnp.bfloat16)
    key_local = projected[..., 1, :].astype(jnp.bfloat16)
    value_local = (projected[..., 2, :] + bias_float[1]).astype(jnp.bfloat16)
    key_clip, value_clip = (
        lax.all_gather(key_local, "seq", axis=1, tiled=True),
        lax.all_gather(value_local, "seq", axis=1, tiled=True),
    )
    query_rows = half_frames * patches_all
    key_rows = key_clip.shape[1] * patches_all
    visible = jnp.maximum(frame_ids[None, :] + 1, context_frames[:, None]).astype(jnp.int32).reshape(-1)
    query_flat = queries.reshape(clip_count, query_rows, head_cols)
    key_flat = key_clip.reshape(clip_count, key_rows, head_cols)
    value_flat = value_clip.reshape(clip_count, key_rows, head_cols)
    attended, weights_low, inverse_mass = attn_fwd(
        visible, query_flat, key_flat, value_flat, patches_all
    )
    attended_rows = attended.reshape(clip_count, half_frames, patches_all, head_cols)
    portion = attended_rows
    branch_rows = lax.psum_scatter(
        jnp.einsum("cfpe,ed->pcfd", portion, w_out, preferred_element_type=jnp.float32).astype(
            jnp.bfloat16
        ),
        "tensor",
        scatter_dimension=0,
        tiled=True,
    ).astype(jnp.float32)
    branch_one = jnp.transpose(branch_rows, (1, 2, 0, 3)) + b_out.astype(jnp.float32)
    hidden_one = block_input + gate_one * branch_one
    normed_two, inverse_two = normalize(hidden_one)
    mlp_in = (normed_two * (1.0 + scale_two) + shift_two).astype(jnp.bfloat16)
    mlp_all = lax.all_gather(mlp_in, "tensor", axis=2, tiled=True)
    pre_act = jnp.einsum(
        "cfpd,de->cfpe", mlp_all, w_up, preferred_element_type=jnp.float32
    ) + b_up.astype(jnp.float32)
    activated = jax.nn.gelu(pre_act, approximate=True).astype(jnp.bfloat16)
    portion = activated
    mlp_rows = lax.psum_scatter(
        jnp.einsum("cfpe,ed->pcfd", portion, w_down, preferred_element_type=jnp.float32).astype(
            jnp.bfloat16
        ),
        "tensor",
        scatter_dimension=0,
        tiled=True,
    ).astype(jnp.float32)
    mlp_out = jnp.transpose(mlp_rows, (1, 2, 0, 3)) + b_down.astype(jnp.float32)
    output = hidden_one + gate_two * mlp_out
    grad_mlp = gate_two * cotangent
    grad_gate_two = jnp.sum(cotangent * mlp_out, axis=2)
    grad_b_down = jnp.sum(grad_mlp, axis=(0, 1, 2))
    grad_mlp_low = grad_mlp.astype(jnp.bfloat16)
    grad_mlp_all = lax.all_gather(grad_mlp_low, "tensor", axis=2, tiled=True)
    grad_act = jnp.einsum("cfpd,ed->cfpe", grad_mlp_all, w_down, preferred_element_type=jnp.float32)
    grad_w_down = jnp.einsum(
        "cfpe,cfpd->ed", activated, grad_mlp_all, preferred_element_type=jnp.float32
    )
    grad_pre = gelu_back(pre_act, grad_act).astype(jnp.bfloat16)
    grad_b_up = jnp.sum(grad_pre.astype(jnp.float32), axis=(0, 1, 2))
    grad_w_up = jnp.einsum("cfpd,cfpe->de", mlp_all, grad_pre, preferred_element_type=jnp.float32)
    portion = grad_pre
    grad_mlp_rows = lax.psum_scatter(
        jnp.einsum("cfpe,de->pcfd", portion, w_up, preferred_element_type=jnp.float32).astype(
            jnp.bfloat16
        ),
        "tensor",
        scatter_dimension=0,
        tiled=True,
    ).astype(jnp.float32)
    grad_mlp_in = jnp.transpose(grad_mlp_rows, (1, 2, 0, 3))
    grad_shift_two = jnp.sum(grad_mlp_in, axis=2)
    grad_scale_two = jnp.sum(grad_mlp_in * normed_two, axis=2)
    grad_hidden = cotangent + norm_back(grad_mlp_in * (1.0 + scale_two), normed_two, inverse_two)
    grad_branch = gate_one * grad_hidden
    grad_gate_one = jnp.sum(grad_hidden * branch_one, axis=2)
    grad_b_out = jnp.sum(grad_branch, axis=(0, 1, 2))
    grad_branch_all = lax.all_gather(grad_branch.astype(jnp.bfloat16), "tensor", axis=2, tiled=True)
    grad_attended = jnp.einsum(
        "cfpd,ed->cfpe", grad_branch_all, w_out, preferred_element_type=jnp.float32
    ).astype(jnp.bfloat16)
    grad_w_out = jnp.einsum(
        "cfpe,cfpd->ed", attended_rows, grad_branch_all, preferred_element_type=jnp.float32
    )
    grad_queries, grad_keys, grad_values = attn_bwd(
        visible,
        query_flat,
        key_flat,
        value_flat,
        attended,
        grad_attended.reshape(clip_count, query_rows, head_cols),
        inverse_mass,
        weights_low,
        patches_all,
    )
    key_shape = (clip_count, key_clip.shape[1], patches_all, head_cols)
    grad_key_own, grad_value_own = (
        lax.psum_scatter(
            grad_keys.reshape(key_shape).astype(jnp.bfloat16),
            "seq",
            scatter_dimension=1,
            tiled=True,
        ).astype(jnp.float32),
        lax.psum_scatter(
            grad_values.reshape(key_shape).astype(jnp.bfloat16),
            "seq",
            scatter_dimension=1,
            tiled=True,
        ).astype(jnp.float32),
    )
    grad_qkv = jnp.stack(
        [
            grad_queries.reshape(clip_count, half_frames, patches_all, head_cols),
            grad_key_own.astype(jnp.bfloat16),
            grad_value_own.astype(jnp.bfloat16),
        ],
        axis=3,
    )
    grad_w_qkv = jnp.einsum(
        "cfpd,cfpke->dke", attn_all, grad_qkv, preferred_element_type=jnp.float32
    )
    grad_qv_bias = jnp.sum(grad_qkv[:, :, :, 0::2, :].astype(jnp.float32), axis=(0, 1, 2))
    portion = grad_qkv
    grad_attn_rows = lax.psum_scatter(
        jnp.einsum("cfpke,dke->pcfd", portion, w_qkv, preferred_element_type=jnp.float32).astype(
            jnp.bfloat16
        ),
        "tensor",
        scatter_dimension=0,
        tiled=True,
    ).astype(jnp.float32)
    grad_attn_in = jnp.transpose(grad_attn_rows, (1, 2, 0, 3))
    grad_shift_one = jnp.sum(grad_attn_in, axis=2)
    grad_scale_one = jnp.sum(grad_attn_in * normed_one, axis=2)
    grad_input = grad_hidden + norm_back(grad_attn_in * (1.0 + scale_one), normed_one, inverse_one)
    grad_modulation = jnp.concatenate(
        [
            grad_shift_one,
            grad_scale_one,
            grad_gate_one,
            grad_shift_two,
            grad_scale_two,
            grad_gate_two,
        ],
        axis=-1,
    )
    grad_modulation = grad_modulation.reshape(clip_count * half_frames, 6 * breadth)
    modulation_cols, out_bias_part, down_bias_part = (
        lax.psum_scatter(
            grad_modulation.astype(jnp.bfloat16), "tensor", scatter_dimension=1, tiled=True
        ).astype(jnp.float32),
        lax.psum_scatter(
            grad_b_out.astype(jnp.bfloat16), "tensor", scatter_dimension=0, tiled=True
        ).astype(jnp.float32),
        lax.psum_scatter(
            grad_b_down.astype(jnp.bfloat16), "tensor", scatter_dimension=0, tiled=True
        ).astype(jnp.float32),
    )
    condition_rows = condition.reshape(clip_count * half_frames, breadth).astype(jnp.float32)
    grad_w_mod = jnp.dot(condition_rows.T, modulation_cols, precision=lax.Precision.HIGHEST)
    grad_b_mod = jnp.sum(modulation_cols, axis=0)
    (
        total_w_qkv,
        total_qv_bias,
        total_w_out,
        total_b_out,
        total_w_up,
        total_b_up,
        total_w_down,
        total_b_down,
        total_w_mod,
        total_b_mod,
    ) = (
        lax.psum(grad_w_qkv.astype(jnp.bfloat16), ("dp", "seq")).astype(jnp.float32),
        lax.psum(grad_qv_bias.astype(jnp.bfloat16), ("dp", "seq")).astype(jnp.float32),
        lax.psum(grad_w_out.astype(jnp.bfloat16), ("dp", "seq")).astype(jnp.float32),
        lax.psum(out_bias_part.astype(jnp.bfloat16), ("dp", "seq")).astype(jnp.float32),
        lax.psum(grad_w_up.astype(jnp.bfloat16), ("dp", "seq")).astype(jnp.float32),
        lax.psum(grad_b_up.astype(jnp.bfloat16), ("dp", "seq")).astype(jnp.float32),
        lax.psum(grad_w_down.astype(jnp.bfloat16), ("dp", "seq")).astype(jnp.float32),
        lax.psum(down_bias_part.astype(jnp.bfloat16), ("dp", "seq")).astype(jnp.float32),
        lax.psum(grad_w_mod.astype(jnp.bfloat16), ("dp", "seq")).astype(jnp.float32),
        lax.psum(grad_b_mod.astype(jnp.bfloat16), ("dp", "seq")).astype(jnp.float32),
    )
    return (
        output,
        grad_input,
        total_w_qkv,
        total_qv_bias,
        total_w_out,
        total_b_out,
        total_w_up,
        total_b_up,
        total_w_down,
        total_b_down,
        total_w_mod,
        total_b_mod,
    )


def solution(mesh):
    placed = (
        P("dp", "seq", "tensor", None),
        P(None, None, "tensor"),
        P(None, "tensor"),
        P("tensor", None),
        P(),
        P(None, "tensor"),
        P("tensor"),
        P("tensor", None),
        P(),
        P(),
        P(),
        P("dp"),
        P("dp", "seq"),
        P("dp", "seq", "tensor", None),
    )
    return jax.shard_map(
        body,
        mesh=mesh,
        in_specs=placed,
        out_specs=(
            P("dp", "seq", "tensor", None),
            P("dp", "seq", "tensor", None),
            P(None, None, "tensor"),
            P(None, "tensor"),
            P("tensor", None),
            P("tensor"),
            P(None, "tensor"),
            P("tensor"),
            P("tensor", None),
            P("tensor"),
            P(None, "tensor"),
            P("tensor"),
        ),
        check_vma=False,
    )
```
